32 devices in a mesh: section: 4 (over y, core), fsdp: 8 (over z, x).
Axes of the slice: x: 2, y: 2, z: 4, core: 2. Of those that a mesh axis runs over, the one named last changes fastest.
Arguments:
- hidden_in: bfloat16 [1024, 4096], P('fsdp'), may hold values from -6 to 6
- out_grad: bfloat16 [1024, 4096], P('fsdp'), may hold values from -6 to 6
- fast_in: float32 [4, 4096, 1024], P('section', 'fsdp'), may hold values from -6 to 6
- fast_out: float32 [4, 1024, 4096], P('section', None, 'fsdp'), may hold values from -6 to 6
- slow_in: float32 [4, 4096, 1024], P('section', 'fsdp'), may hold values from -6 to 6
- slow_out: float32 [4, 1024, 4096], P('section', None, 'fsdp'), may hold values from -6 to 6
Outputs:
- section_out: bfloat16 [4, 1024, 4096], P('section', 'fsdp')
- input_grad: bfloat16 [4, 1024, 4096], P('section', 'fsdp')
- synced_in: float32 [4, 4096, 1024], P('section', 'fsdp')
- synced_out: float32 [4, 1024, 4096], P('section', None, 'fsdp')
The draws below stay inside these ranges and needn't reach their ends.
All inputs are finite; a program needn't handle non-finite values.
Results may differ from the reference program's by a relative error of at most 0.014.
Values may be sent and summed in bfloat16 or wider, within the bound.
No kernel may reach another device: no remote copies, remote signals or barrier semaphores. Data moves between devices by JAX's collectives and lax.ppermute only.
A program may use at most 896 MiB of HBM per device.

```python
import math
import jax
import jax.numpy as jnp
from jax import lax

D = 4096
LAT = 1024
TOK_DEV = 128
TOKENS = 1024
LAYERS = 4
N_SECTION = 4
N_FSDP = 8


def raised(entries, stream_key, source, target, parts, factor):
    owner, partner = [(jnp.arange(entries.shape[axis_at]) // (entries.shape[axis_at] // parts)).reshape([-1 if axis == axis_at else 1 for axis in range(entries.ndim)]) for axis_at in (source, target)]
    chosen = jax.random.permutation(stream_key, parts)[partner]
    strong = (owner == chosen) | (owner == (partner + parts // 2) % parts)
    return jnp.where(strong, factor * entries, entries)


def level_of(stream_key, shape, split, low, largest):
    def one(axis_at, parts):
        steps = jax.random.uniform(jax.random.fold_in(jax.random.fold_in(stream_key, 6), axis_at), (parts,), jnp.float32, low / len(split), largest / len(split))
        return jnp.repeat(jnp.exp(steps), shape[axis_at] // parts).reshape((-1,) + (1,) * (len(shape) - axis_at - 1))

    level = one(*split[0])
    for cut in split[1:]:
        level = level * one(*cut)
    return level


def centred(stream_key, dims, deviation, reach, shards=(), kind=jnp.bfloat16):
    entries = jax.random.normal(stream_key, dims, jnp.float32) * deviation
    if len(shards) > 0:
        entries = level_of(stream_key, dims, shards, -0.22, 0.18) * entries
    return jnp.clip(entries, min=-reach, max=reach).astype(kind)


def gaussian_with(own_key, shape, width, reach, cuts, heavy, kind=jnp.bfloat16):
    array = width * jax.random.normal(own_key, shape, jnp.float32)
    if cuts:
        array = array * level_of(own_key, shape, cuts, -0.22, 0.18)
    return jnp.clip(raised(array, jax.random.fold_in(own_key, 3), *heavy), -reach, reach).astype(kind)


def setup_inputs(seed: int = 0) -> dict:
    seeds = jax.random.split(jax.random.key(seed), 7)
    hidden_in = gaussian_with(seeds[0], (TOKENS, D), 1.0, 6.0, ((0, 8),), (0, 1, 8, 2.0))
    out_grad = centred(seeds[1], (TOKENS, D), 1.0, 6.0, ((0, 8),))
    fast_in = centred(seeds[2], (LAYERS, D, LAT), 1.0, 6.0, ((0, 4), (1, 8)), jnp.float32)
    fast_out = centred(seeds[3], (LAYERS, LAT, D), 1.0, 6.0, ((0, 4), (2, 8)), jnp.float32)
    slow_in = centred(seeds[4], (LAYERS, D, LAT), 1.0, 6.0, ((0, 4), (1, 8)), jnp.float32)
    slow_out = centred(seeds[5], (LAYERS, LAT, D), 1.0, 6.0, ((0, 4), (2, 8)), jnp.float32)
    return {"hidden_in": hidden_in, "out_grad": out_grad, "fast_in": fast_in, "fast_out": fast_out, "slow_in": slow_in, "slow_out": slow_out}


epsilon = 1e-05
fast_rate = 0.5
preview_mix = 0.5

def contract_last(left_rows, right_rows):
    return lax.dot_general(left_rows, right_rows, (((1,), (1,)), ((), ())), preferred_element_type=jnp.float32)

def contract_first(left_rows, right_rows):
    return lax.dot_general(left_rows, right_rows, (((0,), (0,)), ((), ())), preferred_element_type=jnp.float32)

def prepare(hidden, weight_in):
    widened = hidden.astype(jnp.float32)
    inverse_rms = lax.rsqrt(lax.optimization_barrier(jnp.mean(widened * widened, axis=-1, keepdims=True)) + epsilon)
    normed = (widened * inverse_rms).astype(jnp.bfloat16)
    pre_act = jnp.dot(normed, weight_in, preferred_element_type=jnp.float32)
    activated = jax.nn.silu(pre_act).astype(jnp.bfloat16)
    return (widened, inverse_rms, normed, pre_act, activated)

def advance(hidden, weight_in, weight_out):
    widened, inverse_rms, normed, pre_act, activated = prepare(hidden, weight_in)
    return (widened + jnp.dot(activated, weight_out, preferred_element_type=jnp.float32)).astype(jnp.bfloat16)

def retreat(hidden, cot_in, weight_in, weight_out):
    widened, inverse_rms, normed, pre_act, activated = prepare(hidden, weight_in)
    act_grad = contract_last(cot_in, weight_out)
    sigmoid_vals = jax.nn.sigmoid(pre_act)
    pre_grad = (act_grad * sigmoid_vals * (1.0 + pre_act * (1.0 - sigmoid_vals))).astype(jnp.bfloat16)
    norm_grad = contract_last(pre_grad, weight_in)
    unit_rows = widened * inverse_rms
    rms_grad = inverse_rms * (norm_grad - unit_rows * lax.optimization_barrier(jnp.mean(norm_grad * unit_rows, axis=-1, keepdims=True)))
    earlier = (cot_in.astype(jnp.float32) + rms_grad).astype(jnp.bfloat16)
    return (earlier, normed, pre_grad, activated)

def shard_sum(left_rows, right_rows, factor):
    pieces_left = left_rows.reshape(N_FSDP, TOK_DEV, left_rows.shape[1])
    pieces_right = right_rows.reshape(N_FSDP, TOK_DEV, right_rows.shape[1])

    def accumulate(running, operands):
        partial_value = contract_first(operands[0], operands[1]) * factor
        rounded = lax.optimization_barrier(partial_value.astype(jnp.bfloat16))
        return (running + rounded.astype(jnp.float32), None)
    start = jnp.zeros((left_rows.shape[1], right_rows.shape[1]), jnp.float32)
    running, ignored = lax.scan(accumulate, start, (pieces_left, pieces_right))
    return running

def reference(hidden_in, out_grad, fast_in, fast_out, slow_in, slow_out):
    in_scale = 1.0 / math.sqrt(D)
    out_scale = 1.0 / math.sqrt(LAT)
    weights_in = [(fast_in[layer_index] * in_scale).astype(jnp.bfloat16) for layer_index in range(N_SECTION)]
    weights_out = [(fast_out[layer_index] * out_scale).astype(jnp.bfloat16) for layer_index in range(N_SECTION)]
    inputs = []
    outputs = []
    current = hidden_in
    for layer_index in range(N_SECTION):
        inputs.append(current)
        current = advance(current, weights_in[layer_index], weights_out[layer_index])
        outputs.append(current)
    cot_in = out_grad
    cotangents = [None] * N_SECTION
    synced_first = [None] * N_SECTION
    synced_second = [None] * N_SECTION
    for layer_index in reversed(range(N_SECTION)):
        earlier, normed, pre_grad, activated = retreat(inputs[layer_index], cot_in, weights_in[layer_index], weights_out[layer_index])
        grad_in = shard_sum(normed, pre_grad, in_scale)
        grad_out = shard_sum(activated, cot_in, out_scale)
        fresh_in = fast_in[layer_index] - fast_rate * grad_in
        fresh_out = fast_out[layer_index] - fast_rate * grad_out
        synced_first[layer_index] = slow_in[layer_index] + preview_mix * (fresh_in - slow_in[layer_index])
        synced_second[layer_index] = slow_out[layer_index] + preview_mix * (fresh_out - slow_out[layer_index])
        cotangents[layer_index] = earlier
        cot_in = earlier
    return (jnp.stack(outputs), jnp.stack(cotangents), jnp.stack(synced_first), jnp.stack(synced_second))
```

```python
import functools
import math

import jax
import jax.numpy as jnp
from jax import lax
from jax.experimental import pallas as pl
from jax.experimental.pallas import tpu as pltpu
from jax.sharding import PartitionSpec as P

epsilon = 1e-05
fast_rate = 0.5
preview_mix = 0.5
pair = 2
lanes = 128


half_type = jnp.bfloat16
full_type = jnp.float32


def local_call(body, outs, args, flops=0):
    moved = sum(v.size * v.dtype.itemsize for v in list(args) + list(outs))
    return pl.pallas_call(
        body,
        out_shape=outs,
        in_specs=[pl.BlockSpec(memory_space=pltpu.VMEM)] * len(args),
        out_specs=[pl.BlockSpec(memory_space=pltpu.VMEM)] * len(outs),
        cost_estimate=pl.CostEstimate(flops=flops, bytes_accessed=moved, transcendentals=0),
    )(*args)


def shaped(shape, kind=half_type):
    return jax.ShapeDtypeStruct(shape, kind)


def nn(a, b):
    return lax.dot_general(a, b, (((1,), (0,)), ((), ())), preferred_element_type=full_type)


def nt(a, b):
    return lax.dot_general(a, b, (((1,), (1,)), ((), ())), preferred_element_type=full_type)


def tn(a, b):
    return lax.dot_general(a, b, (((0,), (0,)), ((), ())), preferred_element_type=full_type)


def split_columns(total):
    high = total.astype(half_type)
    low = (total - high.astype(full_type)).astype(half_type)
    place = lax.broadcasted_iota(jnp.int32, (total.shape[0], lanes), 1)
    zero = jnp.zeros((total.shape[0], lanes), full_type)
    return jnp.where(
        place == 0,
        high.astype(full_type),
        jnp.where(place == 1, low.astype(full_type), zero),
    ).astype(half_type)


def joined(columns):
    return jnp.sum(columns, axis=1, keepdims=True)


def wide(value):
    return value.astype(full_type)


def stack_rows(refs):
    return jnp.concatenate([ref[...] for ref in refs], axis=0)


def enter_body(count, units, *refs):
    own, other = refs[0], refs[1]
    weights = refs[2 : 2 + count]
    keep, send = refs[2 + count :]
    weight = stack_rows(weights)
    for source, target in ((other, send), (own, keep)):
        rows = source[...]
        target[:, :units] = nn(rows, weight).astype(half_type)
        square = wide(rows) * wide(rows)
        target[:, units:] = split_columns(joined(square))


def step_body(count, units, follow, *refs):
    act_own, act_other, own, other = refs[:4]
    outs = refs[4 + count : 8 + count]
    leave = stack_rows(refs[4 : 4 + count])
    if follow:
        enter = stack_rows(refs[4 + count : 4 + 2 * count])
        outs = refs[4 + 2 * count :]
        next_own, next_other, keep, send = outs
        groups = ((act_other, other, next_other, send), (act_own, own, next_own, keep))
    else:
        next_own, next_other = refs[4 + count :]
        groups = ((act_other, other, next_other, None), (act_own, own, next_own, None))
    for act, before, after, target in groups:
        rows = (wide(before[...]) + nt(act[...], leave)).astype(half_type)
        after[...] = rows
        if target is not None:
            target[:, :units] = nn(rows, enter).astype(half_type)
            square = wide(rows) * wide(rows)
            target[:, units:] = split_columns(joined(square))


def turn_body(count, own, other, *refs):
    weight = stack_rows(refs[:count])
    keep, send = refs[count:]
    send[...] = nn(other[...], weight).astype(half_type)
    keep[...] = nn(own[...], weight).astype(half_type)


def back_body(count, units, follow, *refs):
    q_own, q_other, g_own, g_other, h_own, h_other = refs[:6]
    enter = stack_rows(refs[6 : 6 + count])
    if follow:
        leave = stack_rows(refs[6 + count : 6 + 2 * count])
        next_own, next_other, keep, send = refs[6 + 2 * count :]
    else:
        next_own, next_other = refs[6 + count :]
        keep = send = None
    for q, g, h, after, target in (
        (q_other, g_other, h_other, next_other, send),
        (q_own, g_own, h_own, next_own, keep),
    ):
        factor = joined(wide(q[:, units:]))
        rows = wide(g[...]) + nt(q[:, :units], enter) - wide(h[...]) * factor
        rows = rows.astype(half_type)
        after[...] = rows
        if target is not None:
            target[...] = nn(rows, leave).astype(half_type)


def term_body(count, scale, units, left_own, left_other, right_own, right_other, *outs):
    depth = outs[0].shape[0]
    left = jnp.concatenate([left_own[...], left_other[...]], axis=0)
    right = jnp.concatenate([right_own[:, :units], right_other[:, :units]], axis=0)
    total = (tn(left, right) * scale).astype(half_type)
    for index, out in enumerate(outs):
        out[...] = total[index * depth : (index + 1) * depth]


def merged(first, second, units):
    total = wide(first) + wide(second)
    if first.shape[1] == units:
        return total.astype(half_type)
    return jnp.concatenate(
        [total[:, :units].astype(half_type), split_columns(joined(total[:, units:]))], axis=1
    )


def divide_body(units, keep, got, upper, lower):
    rows = upper.shape[0]
    total = merged(keep[...], got[...], units)
    upper[...] = total[:rows]
    lower[...] = total[rows:]


def both_body(units, a, got_a, b, got_b, out_a, out_b):
    out_a[...] = merged(a[...], got_a[...], units)
    out_b[...] = merged(b[...], got_b[...], units)


def sigmoid(value):
    return 1.0 / (1.0 + jnp.exp(-value))


def gate_body(units, width, a, got_a, b, got_b, pre, rate, act):
    total = jnp.concatenate(
        [wide(a[...]) + wide(got_a[...]), wide(b[...]) + wide(got_b[...])], axis=0
    )
    square = joined(total[:, units:])
    inverse = lax.rsqrt(square / width + epsilon)
    value = total[:, :units] * inverse
    pre[...] = value
    rate[...] = jnp.broadcast_to(inverse, rate.shape)
    act[...] = (value * sigmoid(value)).astype(half_type)


def ungate_body(units, width, a, got_a, b, got_b, pre, rate, q):
    grad = jnp.concatenate(
        [wide(a[...]) + wide(got_a[...]), wide(b[...]) + wide(got_b[...])], axis=0
    )
    value = pre[...]
    inverse = rate[:, :1]
    gate = sigmoid(value)
    pre_grad = grad * gate * (1.0 + value * (1.0 - gate))
    mean = joined(pre_grad * value) / width
    q[:, :units] = (pre_grad * inverse).astype(half_type)
    q[:, units:] = split_columns(inverse * inverse * mean)


def shards(hidden_in, out_grad, fast_in, fast_out, slow_in, slow_out):
    sections = lax.axis_size("section")
    ring = lax.axis_size("fsdp") // pair
    far = sections // 2
    s = lax.axis_index("section")
    f = lax.axis_index("fsdp")
    x, z = f % pair, f // pair
    core = s % 2
    tokens, model_width = hidden_in.shape
    depth, units = fast_in.shape[1:]
    sub = depth // sections
    slice_width = ring * sub
    in_scale = 1.0 / math.sqrt(model_width)
    out_scale = 1.0 / math.sqrt(units)
    layers = range(sections)

    def over_section(value, k, targets=None):
        wanted = layers if targets is None else targets
        return lax.ppermute(
            value, "section", [(i, i ^ k) for i in layers if (i ^ k) in wanted]
        )

    def over_pair(value):
        return lax.ppermute(value, "fsdp", [(i, i ^ 1) for i in range(ring * pair)])

    def over_ring(value, step):
        moves = [
            (place * pair + side, (place + step) % ring * pair + side)
            for place in range(ring)
            for side in range(pair)
        ]
        return lax.ppermute(value, "fsdp", moves)

    def chosen(values, index):
        result = values[0]
        for position in range(1, len(values)):
            result = jnp.where(index == position, values[position], result)
        return result

    local_in = (fast_in[0] * in_scale).astype(half_type)
    local_out = (fast_out[0] * out_scale).astype(half_type).T

    def spread(local):
        got = [lax.dynamic_slice_in_dim(local, s * sub, sub, 0)]
        for k in range(1, sections):
            part = lax.dynamic_slice_in_dim(local, (s ^ k) * sub, sub, 0)
            got.append(over_section(part, k))
        return [chosen(got, s ^ layer) for layer in layers]

    def gather(parts):
        half = ring // 2
        up, down = [parts], [parts]
        for step in range(1, half + 1):
            last = step == half
            send_up = [up[-1][0]] if last else up[-1]
            send_down = [down[-1][1]] if last else down[-1]
            up.append(move(send_up, 1))
            down.append(move(send_down, -1))
        enter, leave = [], []
        for j in range(ring):
            if j < half:
                enter.append(down[j][0])
                leave.append(down[j][1])
            elif j == half:
                enter.append(up[half][0])
                leave.append(down[half][0])
            else:
                enter.append(up[ring - j][0])
                leave.append(up[ring - j][1])
        return enter, leave

    def move(values, step):
        return [over_ring(value, step) for value in values]

    in_parts = spread(local_in)
    out_parts = spread(local_out)
    enters, leaves = [], []
    for layer in layers:
        enter, leave = gather([in_parts[layer], out_parts[layer]])
        enters.append(enter)
        leaves.append(leave)

    def columns(block, side):
        return jnp.concatenate(
            [
                lax.dynamic_slice_in_dim(
                    block, ((z + j) % ring * pair + side) * depth + s * sub, sub, 1
                )
                for j in range(ring)
            ],
            axis=1,
        )

    def to_group(block):
        mine = columns(block, x)
        got = over_pair(columns(block, 1 - x))
        return jnp.where(core == x, mine, got), jnp.where(core == x, got, mine)

    def from_group(own, other):
        mine = jnp.where(core == x, own, other)
        got = over_pair(jnp.where(core == x, other, own))
        return jnp.concatenate([mine, got], axis=1)

    def summed(keep, send):
        got = over_section(send, 1)
        rows, width = keep.shape
        part = shaped((rows // 2, width))
        a, b = local_call(functools.partial(divide_body, units), [part, part], [keep, got])
        got_a, got_b = over_pair(a), over_section(b, far)
        a, b = local_call(
            functools.partial(both_body, units), [part, part], [a, got_a, b, got_b]
        )
        got_a, got_b = over_section(a, far), over_pair(b)
        return [a, got_a, b, got_b]

    slab = shaped((tokens, slice_width))
    wide_slab = shaped((tokens, units + lanes))
    unit_slab = shaped((tokens, units))
    product = 2 * tokens * slice_width * units

    own, other = to_group(hidden_in)
    keep, send = local_call(
        functools.partial(enter_body, ring, units),
        [wide_slab, wide_slab],
        [own, other, *enters[0]],
        2 * product,
    )
    states, saved, produced = [], [], []
    for layer in layers:
        states.append((own, other))
        pre, rate, act = local_call(
            functools.partial(gate_body, units, model_width),
            [shaped((tokens, units), full_type), shaped((tokens, lanes), full_type), unit_slab],
            summed(keep, send),
        )
        act_other = over_section(act, 1)
        saved.append((pre, rate, act, act_other))
        follow = layer + 1 < sections
        args = [act, act_other, own, other, *leaves[layer]]
        if follow:
            own, other, keep, send = local_call(
                functools.partial(step_body, ring, units, True),
                [slab, slab, wide_slab, wide_slab],
                args + enters[layer + 1],
                4 * product,
            )
        else:
            own, other = local_call(
                functools.partial(step_body, ring, units, False), [slab, slab], args, 2 * product
            )
        produced.append(from_group(own, other))

    g_own, g_other = to_group(out_grad)
    keep, send = local_call(
        functools.partial(turn_body, ring),
        [unit_slab, unit_slab],
        [g_own, g_other, *leaves[-1]],
        2 * product,
    )
    piece = shaped((sub, units))

    def terms(scale, left, right):
        return local_call(
            functools.partial(term_body, ring, scale, units), [piece] * ring, [*left, *right],
            2 * product,
        )

    def reduce_ring(grad_in, grad_out):
        half = ring // 2
        up_in = up_out = down_in = down_out = None

        def plus(first, second):
            if second is None:
                return first
            return (wide(first) + wide(second)).astype(half_type)

        for step in range(half, 0, -1):
            up_in = over_ring(plus(grad_in[step], up_in), 1)
            down_out = over_ring(plus(grad_out[ring - step], down_out), -1)
            if step < half:
                up_out = over_ring(plus(grad_out[step], up_out), 1)
                down_in = over_ring(plus(grad_in[ring - step], down_in), -1)
        totals = []
        for first, *rest in ((grad_in[0], up_in, down_in), (grad_out[0], up_out, down_out)):
            total = wide(first)
            for value in rest:
                if value is not None:
                    total = total + wide(value)
            totals.append(total.astype(half_type))
        return totals

    cotangents, gradients = [None] * sections, [None] * sections
    for layer in reversed(layers):
        pre, rate, act, act_other = saved[layer]
        grad_out = terms(out_scale, (g_own, g_other), (act, act_other))
        (q,) = local_call(
            functools.partial(ungate_body, units, model_width),
            [wide_slab],
            [*summed(keep, send), pre, rate],
        )
        q_other = over_section(q, 1)
        args = [q, q_other, g_own, g_other, *states[layer], *enters[layer]]
        if layer > 0:
            g_own, g_other, keep, send = local_call(
                functools.partial(back_body, ring, units, True),
                [slab, slab, unit_slab, unit_slab],
                args + leaves[layer - 1],
                4 * product,
            )
        else:
            g_own, g_other = local_call(
                functools.partial(back_body, ring, units, False), [slab, slab], args, 2 * product
            )
        grad_in = terms(in_scale, states[layer], (q, q_other))
        cotangents[layer] = from_group(g_own, g_other)
        gradients[layer] = reduce_ring(grad_in, grad_out)

    def home(pieces):
        got = [chosen(pieces, s)]
        groups = (list(layers)[far:], list(layers)[:far])
        for k in range(1, sections):
            arrived = []
            for group in groups:
                part = pieces[group[0]]
                for layer in group[1:]:
                    part = jnp.where((s ^ k) == layer, pieces[layer], part)
                arrived.append(over_section(part, k, group))
            got.append(jnp.where(s >= far, arrived[0], arrived[1]))
        return [chosen(got, s ^ source) for source in layers]

    def assemble(pieces):
        parts = [part.reshape(tokens, pair, ring, sub) for part in home(pieces)]
        block = jnp.stack(parts, axis=3)
        block = jnp.where(x == 0, block, jnp.flip(block, axis=1))
        twice = jnp.concatenate([block, block], axis=2)
        block = lax.dynamic_slice_in_dim(twice, (ring - z) % ring, ring, 2)
        return jnp.transpose(block, (0, 2, 1, 3, 4)).reshape(tokens, model_width)

    section_out = assemble(produced)[None]
    input_grad = assemble(cotangents)[None]
    total_in = wide(jnp.concatenate(home([pieces[0] for pieces in gradients]), axis=0))
    total_out = wide(jnp.concatenate(home([pieces[1] for pieces in gradients]), axis=0).T)
    fresh_in = fast_in[0] - fast_rate * total_in
    fresh_out = fast_out[0] - fast_rate * total_out
    synced_first = slow_in[0] + preview_mix * (fresh_in - slow_in[0])
    synced_second = slow_out[0] + preview_mix * (fresh_out - slow_out[0])
    return (section_out, input_grad, synced_first[None], synced_second[None])


def solution(mesh):
    placed = (
        P("fsdp", None),
        P("fsdp", None),
        P("section", "fsdp", None),
        P("section", None, "fsdp"),
        P("section", "fsdp", None),
        P("section", None, "fsdp"),
    )
    return jax.shard_map(
        shards,
        mesh=mesh,
        in_specs=placed,
        out_specs=(
            P("section", "fsdp", None),
            P("section", "fsdp", None),
            P("section", "fsdp", None),
            P("section", None, "fsdp"),
        ),
        check_vma=False,
    )
```

```python
import functools
import math

import jax
import jax.numpy as jnp
from jax import lax
from jax.experimental import pallas as pl
from jax.experimental.pallas import tpu as pltpu
from jax.sharding import PartitionSpec as P

epsilon = 1e-05
fast_rate = 0.5
preview_mix = 0.5
pair = 2
lanes = 128


half_type = jnp.bfloat16
full_type = jnp.float32


def local_call(body, outs, args, flops=0, grant=16):
    parts = [arg[1] if isinstance(arg, tuple) else None for arg in args]
    values = [arg[0] if isinstance(arg, tuple) else arg for arg in args]
    moved = sum(v.size * v.dtype.itemsize for v in values + list(outs))

    def bound(*refs):
        inputs = [ref if part is None else ref.at[part] for ref, part in zip(refs, parts)]
        body(*inputs, *refs[len(parts) :])

    return pl.pallas_call(
        bound,
        out_shape=outs,
        in_specs=[pl.BlockSpec(memory_space=pltpu.VMEM)] * len(values),
        out_specs=[pl.BlockSpec(memory_space=pltpu.VMEM)] * len(outs),
        cost_estimate=pl.CostEstimate(flops=flops, bytes_accessed=moved, transcendentals=0),
        compiler_params=pltpu.CompilerParams(vmem_limit_bytes=grant * 2**20),
    )(*values)


def shaped(shape, kind=half_type):
    return jax.ShapeDtypeStruct(shape, kind)


def nn(a, b):
    return lax.dot_general(a, b, (((1,), (0,)), ((), ())), preferred_element_type=full_type)


def nt(a, b):
    return lax.dot_general(a, b, (((1,), (1,)), ((), ())), preferred_element_type=full_type)


def tn(a, b):
    return lax.dot_general(a, b, (((0,), (0,)), ((), ())), preferred_element_type=full_type)


def split_columns(total):
    high = total.astype(half_type)
    low = (total - high.astype(full_type)).astype(half_type)
    place = lax.broadcasted_iota(jnp.int32, (total.shape[0], lanes), 1)
    zero = jnp.zeros((total.shape[0], lanes), full_type)
    return jnp.where(
        place == 0,
        high.astype(full_type),
        jnp.where(place == 1, low.astype(full_type), zero),
    ).astype(half_type)


def folded(rows):
    square = wide(rows) * wide(rows)
    total = square[:, :lanes]
    for begin in range(lanes, square.shape[1], lanes):
        total = total + square[:, begin : begin + lanes]
    return total.astype(half_type)


def joined(columns):
    return jnp.sum(columns, axis=1, keepdims=True)


def wide(value):
    return value.astype(full_type)


def stack_rows(refs):
    return jnp.concatenate([ref[...] for ref in refs], axis=0)


def enter_body(count, units, *refs):
    own, other = refs[0], refs[1]
    weights = refs[2 : 2 + count]
    keep, send = refs[2 + count :]
    weight = stack_rows(weights)
    for source, target in ((other, send), (own, keep)):
        rows = source[...]
        target[:, :units] = nn(rows, weight).astype(half_type)
        target[:, units:] = folded(rows)


def step_body(count, units, follow, *refs):
    act_own, act_other, own, other = refs[:4]
    outs = refs[4 + count : 8 + count]
    leave = stack_rows(refs[4 : 4 + count])
    if follow:
        enter = stack_rows(refs[4 + count : 4 + 2 * count])
        outs = refs[4 + 2 * count :]
        next_own, next_other, keep, send = outs
        groups = ((act_other, other, next_other, send), (act_own, own, next_own, keep))
    else:
        next_own, next_other = refs[4 + count :]
        groups = ((act_other, other, next_other, None), (act_own, own, next_own, None))
    for act, before, after, target in groups:
        rows = (wide(before[...]) + nt(act[...], leave)).astype(half_type)
        after[...] = rows
        if target is not None:
            target[:, :units] = nn(rows, enter).astype(half_type)
            target[:, units:] = folded(rows)


def turn_body(count, own, other, *refs):
    weight = stack_rows(refs[:count])
    keep, send = refs[count:]
    send[...] = nn(other[...], weight).astype(half_type)
    keep[...] = nn(own[...], weight).astype(half_type)


def back_body(count, units, follow, *refs):
    q_own, q_other, g_own, g_other, h_own, h_other = refs[:6]
    enter = stack_rows(refs[6 : 6 + count])
    if follow:
        leave = stack_rows(refs[6 + count : 6 + 2 * count])
        next_own, next_other, keep, send = refs[6 + 2 * count :]
    else:
        next_own, next_other = refs[6 + count :]
        keep = send = None
    for q, g, h, after, target in (
        (q_other, g_other, h_other, next_other, send),
        (q_own, g_own, h_own, next_own, keep),
    ):
        factor = joined(wide(q[:, units:]))
        rows = wide(g[...]) + nt(q[:, :units], enter) - wide(h[...]) * factor
        rows = rows.astype(half_type)
        after[...] = rows
        if target is not None:
            target[...] = nn(rows, leave).astype(half_type)


def term_body(scales, units, *refs):
    count = len(scales)
    outs = refs[4 * count :]
    depth = outs[0].shape[1]
    for place, scale in enumerate(scales):
        left_own, left_other, right_own, right_other = refs[4 * place : 4 * place + 4]
        left = jnp.concatenate([left_own[...], left_other[...]], axis=0)
        right = jnp.concatenate([right_own[:, :units], right_other[:, :units]], axis=0)
        total = (tn(left, right) * scale).astype(half_type)
        for index, out in enumerate(outs):
            out[place] = total[index * depth : (index + 1) * depth]


def sigmoid(value):
    return 1.0 / (1.0 + jnp.exp(-value))


def gate_body(units, width, a, got_a, b, got_b, pre, rate, act):
    total = jnp.concatenate(
        [wide(a[...]) + wide(got_a[...]), wide(b[...]) + wide(got_b[...])], axis=0
    )
    square = joined(total[:, units:])
    inverse = lax.rsqrt(square / width + epsilon)
    value = total[:, :units] * inverse
    pre[...] = value
    rate[...] = jnp.broadcast_to(inverse, rate.shape)
    act[...] = (value * sigmoid(value)).astype(half_type)


def ungate_body(units, width, a, got_a, b, got_b, pre, rate, q):
    grad = jnp.concatenate(
        [wide(a[...]) + wide(got_a[...]), wide(b[...]) + wide(got_b[...])], axis=0
    )
    value = pre[...]
    inverse = rate[:, :1]
    gate = sigmoid(value)
    pre_grad = grad * gate * (1.0 + value * (1.0 - gate))
    mean = joined(pre_grad * value) / width
    q[:, :units] = (pre_grad * inverse).astype(half_type)
    q[:, units:] = split_columns(inverse * inverse * mean)


def shards(hidden_in, out_grad, fast_in, fast_out, slow_in, slow_out):
    sections = lax.axis_size("section")
    ring = lax.axis_size("fsdp") // pair
    far = sections // 2
    s = lax.axis_index("section")
    f = lax.axis_index("fsdp")
    x, z = f % pair, f // pair
    core = s % 2
    tokens, model_width = hidden_in.shape
    depth, units = fast_in.shape[1:]
    sub = depth // sections
    slice_width = ring * sub
    in_scale = 1.0 / math.sqrt(model_width)
    out_scale = 1.0 / math.sqrt(units)
    layers = range(sections)

    def over_section(value, k, targets=None):
        wanted = layers if targets is None else targets
        return lax.ppermute(
            value, "section", [(i, i ^ k) for i in layers if (i ^ k) in wanted]
        )

    def over_pair(value):
        return lax.ppermute(value, "fsdp", [(i, i ^ 1) for i in range(ring * pair)])

    def over_ring(value, step):
        moves = [
            (place * pair + side, (place + step) % ring * pair + side)
            for place in range(ring)
            for side in range(pair)
        ]
        return lax.ppermute(value, "fsdp", moves)

    def chosen(values, index):
        result = values[0]
        for position in range(1, len(values)):
            result = jnp.where(index == position, values[position], result)
        return result

    local_in = (fast_in[0] * in_scale).astype(half_type)
    local_out = (fast_out[0] * out_scale).astype(half_type).T

    def spread(local):
        got = [lax.dynamic_slice_in_dim(local, s * sub, sub, 0)]
        for k in range(1, sections):
            part = lax.dynamic_slice_in_dim(local, (s ^ k) * sub, sub, 0)
            got.append(over_section(part, k))
        return [chosen(got, s ^ layer) for layer in layers]

    def gather(part, way):
        ahead, behind = [part], [part]
        for _ in range(ring // 2):
            ahead.append(over_ring(ahead[-1], way))
        for _ in range(ring - 1 - ring // 2):
            behind.append(over_ring(behind[-1], -way))
        chunks = [None] * ring
        for step, value in enumerate(ahead):
            chunks[-way * step % ring] = value
        for step, value in enumerate(behind):
            chunks[way * step % ring] = value
        return chunks

    in_parts = spread(local_in)
    out_parts = spread(local_out)

    def bundled(parts, way):
        return gather(jnp.stack(parts), way)

    def taken(chunks, part):
        return [(chunk, part) for chunk in chunks]

    enters = [taken(bundled([in_parts[0]], 1), 0)]
    leaves = [taken(bundled([out_parts[0]], -1), 0)]
    for layer in layers[1:]:
        chunks = bundled([in_parts[layer], out_parts[layer]], 1 if layer % 2 else -1)
        enters.append(taken(chunks, 0))
        leaves.append(taken(chunks, 1))

    def columns(block, side):
        return jnp.concatenate(
            [
                lax.dynamic_slice_in_dim(
                    block, ((z + j) % ring * pair + side) * depth + s * sub, sub, 1
                )
                for j in range(ring)
            ],
            axis=1,
        )

    def to_group(blocks):
        got = over_pair(jnp.stack([columns(block, 1 - x) for block in blocks]))
        groups = []
        for place, block in enumerate(blocks):
            mine = columns(block, x)
            groups.append(
                (jnp.where(core == x, mine, got[place]), jnp.where(core == x, got[place], mine))
            )
        return groups

    def from_group(halves):
        got = over_pair(jnp.stack([jnp.where(core == x, other, own) for own, other in halves]))
        return [
            jnp.concatenate([jnp.where(core == x, own, other), got[place]], axis=1)
            for place, (own, other) in enumerate(halves)
        ]

    def plus(first, second):
        return (wide(first) + wide(second)).astype(half_type)

    def summed(keep, send):
        got = over_section(send, 1)
        rows = keep.shape[0] // 2
        a, b = plus(keep[:rows], got[:rows]), plus(keep[rows:], got[rows:])
        got_a, got_b = over_pair(a), over_section(b, far)
        a, b = plus(a, got_a), plus(b, got_b)
        got_a, got_b = over_section(a, far), over_pair(b)
        return [a, got_a, b, got_b]

    slab = shaped((tokens, slice_width))
    wide_slab = shaped((tokens, units + lanes))
    unit_slab = shaped((tokens, units))
    product = 2 * tokens * slice_width * units

    (own, other), (g_own, g_other) = to_group([hidden_in, out_grad])
    keep, send = local_call(
        functools.partial(enter_body, ring, units),
        [wide_slab, wide_slab],
        [own, other, *enters[0]],
        2 * product,
    )
    states, saved, produced = [], [], []
    for layer in layers:
        states.append((own, other))
        pre, rate, act = local_call(
            functools.partial(gate_body, units, model_width),
            [shaped((tokens, units), full_type), shaped((tokens, lanes), full_type), unit_slab],
            summed(keep, send),
        )
        act_other = over_section(act, 1)
        saved.append((pre, rate, act, act_other))
        follow = layer + 1 < sections
        args = [act, act_other, own, other, *leaves[layer]]
        if follow:
            own, other, keep, send = local_call(
                functools.partial(step_body, ring, units, True),
                [slab, slab, wide_slab, wide_slab],
                args + enters[layer + 1],
                4 * product,
            )
        else:
            own, other = local_call(
                functools.partial(step_body, ring, units, False), [slab, slab], args, 2 * product
            )
        if layer % far == far - 1:
            produced += from_group((states + [(own, other)])[-far:])

    keep, send = local_call(
        functools.partial(turn_body, ring),
        [unit_slab, unit_slab],
        [g_own, g_other, *leaves[-1]],
        2 * product,
    )

    def terms(*entries):
        return local_call(
            functools.partial(term_body, [entry[0] for entry in entries], units),
            [shaped((len(entries), sub, units))] * ring,
            [value for entry in entries for value in (*entry[1], *entry[2])],
            2 * product * len(entries),
        )

    def reduce_ring(pieces, way):
        half = ring // 2
        ahead, behind = pieces[way * half % ring], pieces[-way * (ring - 1 - half) % ring]
        for step in range(half - 1, -1, -1):
            ahead = over_ring(ahead, way)
            if step:
                ahead = plus(pieces[way * step % ring], ahead)
        for step in range(ring - 2 - half, -1, -1):
            behind = over_ring(behind, -way)
            if step:
                behind = plus(pieces[-way * step % ring], behind)
        return (wide(pieces[0]) + wide(ahead) + wide(behind)).astype(half_type)

    def home(pieces, targets, cross=range(1, sections)):
        got = {0: chosen(pieces, s - targets[0])}
        for k in cross:
            got[k] = over_section(chosen(pieces, (s ^ k) - targets[0]), k, targets)
        return [got[k] for k in range(sections)]

    def rows_joined(arrays):
        return jnp.concatenate(arrays, axis=0)

    cotangents, gradients = [None] * sections, [None] * sections
    for layer in reversed(layers):
        pre, rate, act, act_other = saved[layer]
        out_entry = (out_scale, (g_own, g_other), (act, act_other))
        if layer == 0:
            first_out = reduce_ring(terms(out_entry), -1)
        (q,) = local_call(
            functools.partial(ungate_body, units, model_width),
            [wide_slab],
            [*summed(keep, send), pre, rate],
        )
        q_other = over_section(q, 1)
        args = [q, q_other, g_own, g_other, *states[layer], *enters[layer]]
        if layer > 0:
            g_own, g_other, keep, send = local_call(
                functools.partial(back_body, ring, units, True),
                [slab, slab, unit_slab, unit_slab],
                args + leaves[layer - 1],
                4 * product,
            )
        else:
            g_own, g_other = local_call(
                functools.partial(back_body, ring, units, False), [slab, slab], args, 2 * product
            )
        cotangents[layer] = (g_own, g_other)
        in_entry = (in_scale, states[layer], (q, q_other))
        if layer == 0:
            first_in = reduce_ring(terms(in_entry), 1)
        else:
            total = reduce_ring(terms(in_entry, out_entry), 1 if layer % 2 else -1)
            gradients[layer] = total.reshape(2 * sub, units)

    late = from_group(cotangents[1:])
    (early,) = from_group(cotangents[:1])
    cot_home = home([early, *late], layers)
    grad_far = home(gradients[far:], list(layers)[far:])
    grad_one = [home([gradients[layer]], [layer]) for layer in range(1, far)]
    in_zero, out_zero = home([first_in[0]], [0]), home([first_out[0]], [0])
    grad_home = []
    for k in layers:
        value = jnp.where(s >= far, grad_far[k], rows_joined([in_zero[k], out_zero[k]]))
        for layer, got in enumerate(grad_one, 1):
            value = jnp.where(s == layer, got[k], value)
        grad_home.append(value)

    def by_source(got):
        return [chosen(got, s ^ source) for source in layers]

    def assemble(pieces):
        parts = [part.reshape(tokens, pair, ring, sub) for part in by_source(pieces)]
        block = jnp.stack(parts, axis=3)
        block = jnp.where(x == 0, block, jnp.flip(block, axis=1))
        twice = jnp.concatenate([block, block], axis=2)
        block = lax.dynamic_slice_in_dim(twice, (ring - z) % ring, ring, 2)
        return jnp.transpose(block, (0, 2, 1, 3, 4)).reshape(tokens, model_width)

    section_out = assemble(home(produced, layers))[None]
    input_grad = assemble(cot_home)[None]
    grad_parts = by_source(grad_home)
    total_in = wide(rows_joined([part[:sub] for part in grad_parts]))
    total_out = wide(rows_joined([part[sub:] for part in grad_parts]).T)
    fresh_in = fast_in[0] - fast_rate * total_in
    fresh_out = fast_out[0] - fast_rate * total_out
    synced_first = slow_in[0] + preview_mix * (fresh_in - slow_in[0])
    synced_second = slow_out[0] + preview_mix * (fresh_out - slow_out[0])
    return (section_out, input_grad, synced_first[None], synced_second[None])


def solution(mesh):
    placed = (
        P("fsdp", None),
        P("fsdp", None),
        P("section", "fsdp", None),
        P("section", None, "fsdp"),
        P("section", "fsdp", None),
        P("section", None, "fsdp"),
    )
    return jax.shard_map(
        shards,
        mesh=mesh,
        in_specs=placed,
        out_specs=(
            P("section", "fsdp", None),
            P("section", "fsdp", None),
            P("section", "fsdp", None),
            P("section", None, "fsdp"),
        ),
        check_vma=False,
    )
```
